512 devices in a mesh: dp: 64 (over x, z_lo, y), ctx: 8 (over z_hi, core).
Axes of the slice: x: 4, y: 8, z: 8 (z_hi: 4, z_lo: 2; z = z_hi * 2 + z_lo), core: 2. Of those that a mesh axis runs over, the one named last changes fastest.
Arguments:
- queries: bfloat16 [65536, 4096], P(('dp', 'ctx')), may hold values from -150 to 150
- keys: bfloat16 [65536, 512], P(('dp', 'ctx')), may hold values from -4 to 4
- values: bfloat16 [65536, 512], P(('dp', 'ctx')), may hold values from -6 to 6
- lengths: int32 [128], replicated, may hold values from 1 to 2048, 65536 in all
Outputs:
- attended: bfloat16 [65536, 4096], P(('dp', 'ctx'))
The draws below stay inside these ranges and needn't reach their ends.
Inputs may be any that keep to these rules, and one draw needn't show every extreme that they name: lengths of the 128 documents sum to 65536; the largest is exactly 2048.
All inputs are finite; a program needn't handle non-finite values.
Results may differ from the reference program's by a relative error of at most 0.0045.
Values may be sent and summed in bfloat16 or wider, within the bound.
A program may use at most 128 MiB of HBM per device.

```python
import math
import jax
import jax.numpy as jnp
import numpy as np
from jax import lax

HEAD_SIZE = 128
QUERY_HEADS = 32
KEY_VALUE_HEADS = 4
DEVICE_TOKENS = 128
LONGEST_LENGTH = 2048
STREAM_TOKENS = 65536
NDOCS = 128


def draw_pair(key):
    key_query = jax.random.fold_in(key, 11)
    key_random_keys = jax.random.fold_in(key, 12)
    key_layout = jax.random.truncated_normal(key_random_keys, -4.0, 4.0, (STREAM_TOKENS, KEY_VALUE_HEADS, HEAD_SIZE), jnp.float32)
    query_layout = 2.5 * jax.random.truncated_normal(key_query, -6.0, 6.0, (STREAM_TOKENS, QUERY_HEADS, HEAD_SIZE), jnp.float32)
    return (query_layout.reshape(STREAM_TOKENS, QUERY_HEADS * HEAD_SIZE), key_layout.reshape(STREAM_TOKENS, KEY_VALUE_HEADS * HEAD_SIZE))


def draw_queries(key, part):
    return draw_pair(key)[0].astype(jnp.bfloat16)


def draw_keys(key, part):
    return draw_pair(key)[1].astype(jnp.bfloat16)


def steps_of(rng, shape, cuts, low, top_value):
    level, own = 1.0, jax.random.fold_in(rng, 6)
    for dim, shards_of in cuts:
        steps = jnp.exp(jax.random.uniform(jax.random.fold_in(own, dim), (shards_of,), jnp.float32, low / len(cuts), top_value / len(cuts)))
        level = level * jnp.repeat(steps, shape[dim] // shards_of).reshape([-1 if axis == dim else 1 for axis in range(len(shape))])
    return level


def profile(amount, total, reach, lean):
    portions = [(1 << 20) // math.isqrt(grade ** lean) + 1 for grade in range(2, amount + 1)]
    surplus, counts = total - reach - (amount - 1), [1] * (amount - 1)
    while surplus > 0:
        movable = [i for i in range(amount - 1) if counts[i] < reach]
        whole, budget = sum([portions[i] for i in movable]), surplus
        for i in movable:
            addition = min(reach - counts[i], max(1, budget * portions[i] // whole), surplus)
            counts[i] = counts[i] + addition
            surplus = surplus - addition
    return np.array([reach] + counts)


def uneven(own_key, amount, total, most, lean):
    if amount == 2:
        one = jax.random.randint(own_key, (), max(1, total - most), min(most, total - 1) + 1)
        return jnp.stack([one, total - one])
    sizes = jnp.asarray(profile(amount, total, most, lean), jnp.int32)
    twos = (amount - 1) // 2
    source_of, receiver = sizes[1:1 + 2 * twos:2], sizes[2:2 + 2 * twos:2]
    slack = jnp.minimum(source_of - 1, most - receiver)
    passed = jax.random.randint(jax.random.fold_in(own_key, 1), (twos,), 0, 1 << 20) % (slack + 1)
    sizes = sizes.at[1:1 + 2 * twos:2].set(source_of - passed).at[2:2 + 2 * twos:2].set(receiver + passed)
    return sizes[jax.random.permutation(jax.random.fold_in(own_key, 2), amount)]


def bell_draw(rng, extent, width, limit, shards=(), held_as=jnp.bfloat16):
    factor_of = steps_of(rng, extent, shards, -0.22, 0.18) if shards else 1.0
    entries = jax.random.normal(rng, extent, jnp.float32) * width * factor_of
    return jnp.minimum(jnp.maximum(entries, -limit), limit).astype(held_as)


def setup_inputs(seed: int = 0) -> dict:
    arg_keys = jax.random.split(jax.random.key(seed), 5)
    return {
        "queries": draw_queries(jax.random.fold_in(arg_keys[4], 71), 0),
        "keys": draw_keys(jax.random.fold_in(arg_keys[4], 71), 0),
        "values": bell_draw(arg_keys[2], (STREAM_TOKENS, KEY_VALUE_HEADS * HEAD_SIZE), 1.0, 6.0, ((0, 512),)),
        "lengths": uneven(arg_keys[3], NDOCS, STREAM_TOKENS, LONGEST_LENGTH, 2).astype(jnp.int32),
    }


def document_of(position, doc_bounds):
    return jnp.sum((position[:, None] >= doc_bounds[None, :]).astype(jnp.int32), axis=1)


def reference(queries, keys, values, lengths):
    doc_bounds = jnp.cumsum(lengths).astype(jnp.int32)
    visible_span = LONGEST_LENGTH + DEVICE_TOKENS
    query_group_width = QUERY_HEADS // KEY_VALUE_HEADS
    scaling = 1.0 / (HEAD_SIZE ** 0.5)
    padded_keys = jnp.concatenate([jnp.zeros((LONGEST_LENGTH, KEY_VALUE_HEADS * HEAD_SIZE), keys.dtype), keys], axis=0)
    padded_values = jnp.concatenate([jnp.zeros((LONGEST_LENGTH, KEY_VALUE_HEADS * HEAD_SIZE), values.dtype), values], axis=0)

    def one_block(block_id):
        leading_entry = (block_id * DEVICE_TOKENS).astype(jnp.int32)
        query_row_slice = lax.dynamic_slice_in_dim(queries, leading_entry, DEVICE_TOKENS, 0)
        query_row_slice = query_row_slice.reshape(DEVICE_TOKENS, KEY_VALUE_HEADS, query_group_width, HEAD_SIZE).astype(jnp.float32)
        key_row_slice = lax.dynamic_slice_in_dim(padded_keys, leading_entry, visible_span, 0).reshape(visible_span, KEY_VALUE_HEADS, HEAD_SIZE).astype(jnp.float32)
        value_row_slice = lax.dynamic_slice_in_dim(padded_values, leading_entry, visible_span, 0).reshape(visible_span, KEY_VALUE_HEADS, HEAD_SIZE).astype(jnp.float32)
        query_pos = leading_entry + jnp.arange(DEVICE_TOKENS, dtype=jnp.int32)
        key_pos = leading_entry - LONGEST_LENGTH + jnp.arange(visible_span, dtype=jnp.int32)
        allowed = (key_pos[None, :] <= query_pos[:, None]) & (key_pos[None, :] >= 0)
        allowed = allowed & (document_of(key_pos, doc_bounds)[None, :] == document_of(query_pos, doc_bounds)[:, None])
        scores = jnp.einsum("qhgd,khd->hgqk", query_row_slice, key_row_slice) * scaling
        scores = jnp.where(allowed, scores, jnp.float32(-1e30))
        rowmax = jnp.max(scores, axis=-1, keepdims=True)
        expwts = jnp.where(allowed, jnp.exp(scores - rowmax), jnp.float32(0.0))
        total = jnp.sum(expwts, axis=-1)
        weights = expwts.astype(jnp.bfloat16).astype(jnp.float32)
        summed = jnp.einsum("hgqk,khd->hgqd", weights, value_row_slice)
        result = summed / total[..., None]
        return jnp.transpose(result, (2, 0, 1, 3)).reshape(DEVICE_TOKENS, QUERY_HEADS * HEAD_SIZE).astype(jnp.bfloat16)

    blocks = lax.map(one_block, jnp.arange(STREAM_TOKENS // DEVICE_TOKENS, dtype=jnp.int32))
    return blocks.reshape(STREAM_TOKENS, QUERY_HEADS * HEAD_SIZE)
```

```python
import functools
import math

import jax
import jax.numpy as jnp
from jax import lax
from jax.experimental import pallas as pl
from jax.experimental.pallas import tpu as pltpu
from jax.sharding import PartitionSpec as P

HEAD_SIZE = 128
QUERY_HEADS = 32
KEY_VALUE_HEADS = 4
GROUP = QUERY_HEADS // KEY_VALUE_HEADS
BLOCK = 128
SLOTS = 9
STACK = 2
NEG = -1e30
EXPONENT_SCALE = math.log2(math.e) / math.sqrt(HEAD_SIZE)
MESH = pl.DeviceIdType.MESH


def kernel(
    dp_size, columns,
    q_hbm, k_hbm, v_hbm, len_ref, out_ref,
    window, q_ref, hot_ref, qmask_ref, max_ref, acc_ref,
    load_sem, recv_sem, pair_recv_sem, row_send_sem, column_send_sem, pair_send_sem,
):
    row = lax.axis_index("dp")
    ctx = lax.axis_index("ctx")
    column, core = ctx // 2, ctx % 2
    chip = row * columns + column
    next_row, last_row = (row + 1) % dp_size, (row + dp_size - 1) % dp_size
    pair = (row, column * 2 + 1 - core)

    def in_row(step):
        return (row, ((column + step) % columns) * 2 + core)

    load_k = pltpu.make_async_copy(k_hbm, window.at[0, core, 0], load_sem.at[0])
    load_v = pltpu.make_async_copy(v_hbm, window.at[0, core, 1], load_sem.at[1])
    load_q = pltpu.make_async_copy(q_hbm, q_ref, load_sem.at[2])
    load_k.start()
    load_v.start()
    load_q.start()

    barrier = pltpu.get_barrier_semaphore()
    partners = [in_row(step) for step in range(1, columns)]
    partners += [(next_row, ctx), (last_row, ctx), pair]
    for partner in partners:
        pl.semaphore_signal(barrier, inc=1, device_id=partner, device_id_type=MESH)
    pl.semaphore_wait(barrier, len(partners))

    def along_rows(slot):
        return pltpu.make_async_remote_copy(
            src_ref=window.at[slot, core],
            dst_ref=window.at[slot + columns, core],
            send_sem=row_send_sem.at[slot],
            recv_sem=recv_sem.at[slot + columns],
            device_id=(next_row, ctx),
            device_id_type=MESH,
        )

    def along_columns(step):
        source = jnp.where(column + step < columns, 0, columns)
        return pltpu.make_async_remote_copy(
            src_ref=window.at[source, core],
            dst_ref=window.at[step, core],
            send_sem=column_send_sem.at[step],
            recv_sem=recv_sem.at[step],
            device_id=in_row(step),
            device_id_type=MESH,
        )

    def to_pair(slot):
        return pltpu.make_async_remote_copy(
            src_ref=window.at[slot, core],
            dst_ref=window.at[slot, core],
            send_sem=pair_send_sem.at[slot],
            recv_sem=pair_recv_sem.at[slot],
            device_id=pair,
            device_id_type=MESH,
        )

    def arrived(slot):
        pltpu.make_async_copy(
            window.at[slot, core], window.at[slot, core], recv_sem.at[slot]
        ).wait()

    def pair_arrived(slot):
        pltpu.make_async_copy(
            window.at[slot, 1 - core], window.at[slot, 1 - core], pair_recv_sem.at[slot]
        ).wait()

    load_k.wait()
    load_v.wait()
    along_rows(0).start()
    for step in range(1, columns):
        @pl.when(column + step < columns)
        def _():
            along_columns(step).start()
    to_pair(0).start()

    lengths = len_ref[...].astype(jnp.float32)
    ndocs = lengths.shape[1]
    sub = lax.broadcasted_iota(jnp.int32, (ndocs, ndocs), 0)
    lane = lax.broadcasted_iota(jnp.int32, (ndocs, ndocs), 1)
    as_column = jnp.sum(jnp.where(sub == lane, lengths, 0.0), axis=1, keepdims=True)
    ends = jnp.sum(jnp.where(sub <= lane, as_column, 0.0), axis=0, keepdims=True)
    begins = ends - lengths
    ends = ends.astype(jnp.int32)
    begins = begins.astype(jnp.int32)
    query_pos = (chip * 2 + core) * BLOCK + lax.broadcasted_iota(jnp.int32, (BLOCK, ndocs), 0)
    same = (query_pos >= begins) & (query_pos < ends)
    qmask_ref[...] = jnp.where(same, 0.0, NEG).astype(jnp.bfloat16)

    @pl.loop(0, SLOTS)
    def _(slot):
        key_pos = (chip - slot) * (2 * BLOCK) + lax.broadcasted_iota(
            jnp.int32, (2 * BLOCK, ndocs), 0
        )
        inside = ((key_pos >= begins) & (key_pos < ends)) | (key_pos < 0)
        hot_ref[slot] = jnp.where(inside, 1.0, 0.0).astype(jnp.bfloat16)

    load_q.wait()

    def attend(slots, first, last):
        count = 2 * BLOCK * len(slots)

        @pl.loop(0, KEY_VALUE_HEADS)
        def _(head):
            lanes = pl.ds(pl.multiple_of(head * HEAD_SIZE, HEAD_SIZE), HEAD_SIZE)
            key = jnp.concatenate([window[s, p, 0, :, lanes] for s in slots for p in (0, 1)], axis=0)
            hot = jnp.concatenate([hot_ref[s] for s in slots], axis=0)
            key = jnp.concatenate([key, hot], axis=1)
            value = jnp.concatenate([window[s, p, 1, :, lanes] for s in slots for p in (0, 1)], axis=0)
            value = jnp.concatenate([value, jnp.ones((count, HEAD_SIZE), jnp.bfloat16)], axis=1)
            for inner in range(0, GROUP, STACK):
                heads = [head * GROUP + inner + i for i in range(STACK)]
                spans = [
                    pl.ds(pl.multiple_of(n * HEAD_SIZE, HEAD_SIZE), HEAD_SIZE) for n in heads
                ]
                query = jnp.concatenate([q_ref[:, span] for span in spans], axis=0)
                mask = jnp.concatenate([qmask_ref[...]] * STACK, axis=0)
                query = jnp.concatenate([query, mask], axis=1)
                scores = lax.dot_general(
                    query, key, (((1,), (1,)), ((), ())), preferred_element_type=jnp.float32
                )
                rows = pl.ds(
                    pl.multiple_of(heads[0] * BLOCK, STACK * BLOCK), STACK * BLOCK
                )
                if first:
                    key_at = lax.broadcasted_iota(jnp.int32, scores.shape, 1)
                    query_at = lax.broadcasted_iota(jnp.int32, scores.shape, 0) % BLOCK
                    scores = jnp.where(key_at <= query_at + core * BLOCK, scores, NEG)
                top = jnp.max(scores, axis=1, keepdims=True)
                if first:
                    top = jnp.broadcast_to(top, (STACK * BLOCK, HEAD_SIZE))
                else:
                    old = max_ref[rows, :]
                    top = jnp.maximum(old, top)
                wide = jnp.concatenate([top] * (count // HEAD_SIZE), axis=1)
                weights = jnp.exp2((scores - wide) * EXPONENT_SCALE).astype(jnp.bfloat16)
                total = jnp.dot(weights, value, preferred_element_type=jnp.float32)
                if not first:
                    rescale = jnp.exp2((old - top) * EXPONENT_SCALE)
                    total = acc_ref[rows, :] * jnp.concatenate([rescale] * 2, axis=1) + total
                if last:
                    result = (total[:, :HEAD_SIZE] / total[:, HEAD_SIZE:]).astype(jnp.bfloat16)
                    for i, span in enumerate(spans):
                        out_ref[:, span] = result[i * BLOCK:(i + 1) * BLOCK, :]
                else:
                    acc_ref[rows, :] = total
                    max_ref[rows, :] = top

    pair_arrived(0)
    attend([0], True, False)

    arrived(columns)
    for step in range(1, columns):
        @pl.when(column + step >= columns)
        def _():
            along_columns(step).start()
    along_rows(columns).start()
    to_pair(columns).start()
    for slot in range(1, columns):
        arrived(slot)
        along_rows(slot).start()
        to_pair(slot).start()

    def middle(turn, carry):
        one, two = 2 * turn + 1, 2 * turn + 2

        @pl.when(turn == 2)
        def _():
            for slot in (one, two):
                arrived(slot)
                to_pair(slot).start()

        pair_arrived(one)
        pair_arrived(two)
        attend([one, two], False, False)
        return carry

    lax.fori_loop(0, 3, middle, 0)
    for slot in (7, 8):
        arrived(slot)
        to_pair(slot).start()
    pair_arrived(7)
    pair_arrived(8)
    attend([7, 8], False, True)

    for slot in range(columns + 1):
        along_rows(slot).wait_send()
    for step in range(1, columns):
        along_columns(step).wait_send()
    for slot in range(SLOTS):
        to_pair(slot).wait_send()


def per_device(queries, keys, values, lengths):
    columns = lax.axis_size("ctx") // 2
    dp_size = lax.axis_size("dp")
    rows = queries.shape[0]
    kv_width = keys.shape[1]
    ndocs = lengths.shape[0]
    any_space = pl.BlockSpec(memory_space=pl.ANY)
    vmem = pl.BlockSpec(memory_space=pltpu.VMEM)
    flops = 4 * rows * QUERY_HEADS * SLOTS * 2 * BLOCK * 2 * HEAD_SIZE
    return pl.pallas_call(
        functools.partial(kernel, dp_size, columns),
        out_shape=jax.ShapeDtypeStruct(queries.shape, jnp.bfloat16),
        in_specs=[any_space, any_space, any_space, vmem],
        out_specs=vmem,
        scratch_shapes=[
            pltpu.VMEM((SLOTS, 2, 2, BLOCK, kv_width), jnp.bfloat16),
            pltpu.VMEM(queries.shape, jnp.bfloat16),
            pltpu.VMEM((SLOTS, 2 * BLOCK, ndocs), jnp.bfloat16),
            pltpu.VMEM((BLOCK, ndocs), jnp.bfloat16),
            pltpu.VMEM((QUERY_HEADS * BLOCK, HEAD_SIZE), jnp.float32),
            pltpu.VMEM((QUERY_HEADS * BLOCK, 2 * HEAD_SIZE), jnp.float32),
            pltpu.SemaphoreType.DMA((3,)),
            pltpu.SemaphoreType.DMA((SLOTS,)),
            pltpu.SemaphoreType.DMA((SLOTS,)),
            pltpu.SemaphoreType.DMA((SLOTS,)),
            pltpu.SemaphoreType.DMA((columns,)),
            pltpu.SemaphoreType.DMA((SLOTS,)),
        ],
        compiler_params=pltpu.CompilerParams(
            collective_id=0, has_side_effects=True, vmem_limit_bytes=48 * 1024 * 1024
        ),
        cost_estimate=pl.CostEstimate(
            flops=flops, bytes_accessed=4 * queries.size, transcendentals=0
        ),
    )(queries, keys, values, lengths.reshape(1, ndocs))


def solution(mesh):
    in_specs = (P(("dp", "ctx"), None), P(("dp", "ctx"), None), P(("dp", "ctx"), None), P())
    out_specs = P(("dp", "ctx"), None)
    return jax.shard_map(
        per_device, mesh=mesh, in_specs=in_specs, out_specs=out_specs, check_vma=False
    )
```

```python
import functools
import math

import jax
import jax.numpy as jnp
from jax import lax
from jax.experimental import pallas as pl
from jax.experimental.pallas import tpu as pltpu
from jax.sharding import PartitionSpec as P

HEAD_SIZE = 128
QUERY_HEADS = 32
KEY_VALUE_HEADS = 4
GROUP = QUERY_HEADS // KEY_VALUE_HEADS
BLOCK = 128
SLOTS = 9
TURN = 8
RELAYED = 2
STACK = 2
DIRECT = KEY_VALUE_HEADS - RELAYED
NEG = -1e30
EXPONENT_SCALE = math.log2(math.e) / math.sqrt(HEAD_SIZE)
MESH = pl.DeviceIdType.MESH


def kernel(
    dp_size, columns, turn,
    q_hbm, k_hbm, v_hbm, len_ref, out_ref,
    window, relay, q_ref, hot_ref, qmask_ref, max_ref, acc_ref,
    load_sem, query_sem, recv_sem, relay_recv_sem, pair_recv_sem, row_send_sem, relay_send_sem, column_send_sem, pair_send_sem,
):
    row = lax.axis_index("dp")
    ctx = lax.axis_index("ctx")
    column, core = ctx // 2, ctx % 2
    chip = row * columns + column
    next_row, last_row = (row + 1) % dp_size, (row + dp_size - 1) % dp_size
    pair = (row, column * 2 + 1 - core)

    def beside(of_row):
        return of_row + turn - 2 * turn * (of_row // turn % 2)

    at_turn = row % turn == turn - 1
    relay_to = (beside(row), ctx)
    relayed_to = ((beside(row) + 1) % dp_size, ctx)
    relayed_from = (beside(last_row), ctx)

    def in_row(step):
        return (row, ((column + step) % columns) * 2 + core)

    def load(part, source, head):
        return pltpu.make_async_copy(
            source.at[:, head * HEAD_SIZE:(head + 1) * HEAD_SIZE],
            window.at[0, core, head, part],
            load_sem.at[part, head],
        )

    for head in range(KEY_VALUE_HEADS):
        load(0, k_hbm, head).start()
        load(1, v_hbm, head).start()
    load_q = pltpu.make_async_copy(q_hbm, q_ref, query_sem)
    load_q.start()

    barrier = pltpu.get_barrier_semaphore()
    partners = [in_row(step) for step in range(1, columns)]
    partners += [(next_row, ctx), (last_row, ctx), pair]
    partners += [relay_to, relayed_to, relayed_from]
    for partner in partners:
        pl.semaphore_signal(barrier, inc=1, device_id=partner, device_id_type=MESH)
    pl.semaphore_wait(barrier, len(partners))

    def along_rows(slot, head):
        return pltpu.make_async_remote_copy(
            src_ref=window.at[slot, core, head],
            dst_ref=window.at[slot + columns, core, head],
            send_sem=row_send_sem.at[slot, head],
            recv_sem=recv_sem.at[slot + columns, head],
            device_id=(next_row, ctx),
            device_id_type=MESH,
        )

    def to_relay(slot, head):
        return pltpu.make_async_remote_copy(
            src_ref=window.at[slot, core, head],
            dst_ref=relay.at[slot, head - DIRECT],
            send_sem=row_send_sem.at[slot, head],
            recv_sem=relay_recv_sem.at[slot, head - DIRECT],
            device_id=relay_to,
            device_id_type=MESH,
        )

    def from_relay(slot, head):
        return pltpu.make_async_remote_copy(
            src_ref=relay.at[slot, head - DIRECT],
            dst_ref=window.at[slot + columns, core, head],
            send_sem=relay_send_sem.at[slot, head - DIRECT],
            recv_sem=recv_sem.at[slot + columns, head],
            device_id=relayed_to,
            device_id_type=MESH,
        )

    def send_along_rows(slot, head):
        relayed = at_turn & (head >= DIRECT)

        @pl.when(relayed)
        def _():
            to_relay(slot, head).start()

        @pl.when(jnp.logical_not(relayed))
        def _():
            along_rows(slot, head).start()

    def pass_relayed(slot, head):
        @pl.when(at_turn & (head >= DIRECT))
        def _():
            piece = relay.at[slot, head - DIRECT]
            pltpu.make_async_copy(piece, piece, relay_recv_sem.at[slot, head - DIRECT]).wait()
            from_relay(slot, head).start()

    def along_columns(step, head):
        source = jnp.where(column + step < columns, 0, columns)
        return pltpu.make_async_remote_copy(
            src_ref=window.at[source, core, head],
            dst_ref=window.at[step, core, head],
            send_sem=column_send_sem.at[step, head],
            recv_sem=recv_sem.at[step, head],
            device_id=in_row(step),
            device_id_type=MESH,
        )

    def to_pair(slot, head):
        return pltpu.make_async_remote_copy(
            src_ref=window.at[slot, core, head],
            dst_ref=window.at[slot, core, head],
            send_sem=pair_send_sem.at[slot, head],
            recv_sem=pair_recv_sem.at[slot, head],
            device_id=pair,
            device_id_type=MESH,
        )

    def arrived(slot, head):
        piece = window.at[slot, core, head]
        pltpu.make_async_copy(piece, piece, recv_sem.at[slot, head]).wait()

    def pair_arrived(slot, head):
        piece = window.at[slot, 1 - core, head]
        pltpu.make_async_copy(piece, piece, pair_recv_sem.at[slot, head]).wait()

    for head in range(KEY_VALUE_HEADS):
        load(0, k_hbm, head).wait()
        load(1, v_hbm, head).wait()
        if head >= DIRECT:
            send_along_rows(0, head)
        else:
            along_rows(0, head).start()
        for step in (1, 3, 2):
            @pl.when(column + step < columns)
            def _():
                along_columns(step, head).start()
        to_pair(0, head).start()

    lengths = len_ref[...].astype(jnp.float32)
    ndocs = lengths.shape[1]
    sub = lax.broadcasted_iota(jnp.int32, (ndocs, ndocs), 0)
    lane = lax.broadcasted_iota(jnp.int32, (ndocs, ndocs), 1)
    as_column = jnp.sum(jnp.where(sub == lane, lengths, 0.0), axis=1, keepdims=True)
    ends = jnp.sum(jnp.where(sub <= lane, as_column, 0.0), axis=0, keepdims=True)
    begins = ends - lengths
    ends = ends.astype(jnp.int32)
    begins = begins.astype(jnp.int32)
    query_pos = (chip * 2 + core) * BLOCK + lax.broadcasted_iota(jnp.int32, (BLOCK, ndocs), 0)
    same = (query_pos >= begins) & (query_pos < ends)
    qmask_ref[...] = jnp.where(same, 0.0, NEG).astype(jnp.bfloat16)

    @pl.loop(0, SLOTS)
    def _(slot):
        key_pos = (chip - slot) * (2 * BLOCK) + lax.broadcasted_iota(
            jnp.int32, (2 * BLOCK, ndocs), 0
        )
        inside = ((key_pos >= begins) & (key_pos < ends)) | (key_pos < 0)
        hot_ref[slot] = jnp.where(inside, 1.0, 0.0).astype(jnp.bfloat16)

    load_q.wait()

    def attend(slots, head, first, last):
        count = 2 * BLOCK * len(slots)
        blocks = [(s, p) for s in slots for p in (0, 1)]
        key = jnp.concatenate([window[s, p, head, 0] for s, p in blocks], axis=0)
        hot = jnp.concatenate([hot_ref[s] for s in slots], axis=0)
        key = jnp.concatenate([key, hot], axis=1)
        value = jnp.concatenate([window[s, p, head, 1] for s, p in blocks], axis=0)
        value = jnp.concatenate([value, jnp.ones((count, HEAD_SIZE), jnp.bfloat16)], axis=1)
        for inner in range(0, GROUP, STACK):
            heads = [head * GROUP + inner + i for i in range(STACK)]
            spans = [
                pl.ds(pl.multiple_of(n * HEAD_SIZE, HEAD_SIZE), HEAD_SIZE) for n in heads
            ]
            query = jnp.concatenate([q_ref[:, span] for span in spans], axis=0)
            mask = jnp.concatenate([qmask_ref[...]] * STACK, axis=0)
            query = jnp.concatenate([query, mask], axis=1)
            scores = lax.dot_general(
                query, key, (((1,), (1,)), ((), ())), preferred_element_type=jnp.float32
            )
            rows = pl.ds(
                pl.multiple_of(heads[0] * BLOCK, STACK * BLOCK), STACK * BLOCK
            )
            if first:
                key_at = lax.broadcasted_iota(jnp.int32, scores.shape, 1)
                query_at = lax.broadcasted_iota(jnp.int32, scores.shape, 0) % BLOCK
                scores = jnp.where(key_at <= query_at + core * BLOCK, scores, NEG)
            top = jnp.max(scores, axis=1, keepdims=True)
            if first:
                top = jnp.broadcast_to(top, (STACK * BLOCK, HEAD_SIZE))
            else:
                old = max_ref[rows, :]
                top = jnp.maximum(old, top)
            wide = jnp.concatenate([top] * (count // HEAD_SIZE), axis=1)
            weights = jnp.exp2((scores - wide) * EXPONENT_SCALE).astype(jnp.bfloat16)
            total = jnp.dot(weights, value, preferred_element_type=jnp.float32)
            if not first:
                rescale = jnp.exp2((old - top) * EXPONENT_SCALE)
                total = acc_ref[rows, :] * jnp.concatenate([rescale] * 2, axis=1) + total
            if last:
                result = (total[:, :HEAD_SIZE] / total[:, HEAD_SIZE:]).astype(jnp.bfloat16)
                for i, span in enumerate(spans):
                    out_ref[:, span] = result[i * BLOCK:(i + 1) * BLOCK, :]
            else:
                acc_ref[rows, :] = total
                max_ref[rows, :] = top

    def own(head, carry):
        pair_arrived(0, head)
        attend([0], head, True, False)
        return carry

    def pass_on(head, carry):
        arrived(columns, head)
        for step in (1, 3, 2):
            @pl.when(column + step >= columns)
            def _():
                along_columns(step, head).start()
        send_along_rows(columns, head)
        to_pair(columns, head).start()
        pass_relayed(0, head)
        return carry

    def middle(head, carry):
        for slot in (1, 3, 2):
            arrived(slot, head)
            send_along_rows(slot, head)
            to_pair(slot, head).start()
        pass_relayed(columns, head)
        for slot in (1, 3, 2):
            pass_relayed(slot, head)
        arrived(8, head)
        to_pair(8, head).start()
        for pair_slots in ([4, 8], [1, 2]):
            for slot in pair_slots:
                pair_arrived(slot, head)
            attend(pair_slots, head, False, False)
        return carry

    def final(head, carry):
        for slot in (5, 7, 6):
            arrived(slot, head)
            to_pair(slot, head).start()
        for slot in (3, 5):
            pair_arrived(slot, head)
        attend([3, 5], head, False, False)
        for slot in (6, 7):
            pair_arrived(slot, head)
        attend([6, 7], head, False, True)
        return carry

    lax.fori_loop(0, KEY_VALUE_HEADS, own, 0)
    lax.fori_loop(0, KEY_VALUE_HEADS, pass_on, 0)
    lax.fori_loop(0, KEY_VALUE_HEADS, middle, 0)
    lax.fori_loop(0, KEY_VALUE_HEADS, final, 0)

    def drain(head, carry):
        for slot in range(columns + 1):
            along_rows(slot, head).wait_send()
        for step in range(1, columns):
            along_columns(step, head).wait_send()

        @pl.when(at_turn & (head >= DIRECT))
        def _():
            for slot in range(columns + 1):
                from_relay(slot, head).wait_send()

        for slot in range(SLOTS):
            to_pair(slot, head).wait_send()
        return carry

    lax.fori_loop(0, KEY_VALUE_HEADS, drain, 0)


def per_device(queries, keys, values, lengths):
    columns = lax.axis_size("ctx") // 2
    dp_size = lax.axis_size("dp")
    rows = queries.shape[0]
    ndocs = lengths.shape[0]
    any_space = pl.BlockSpec(memory_space=pl.ANY)
    vmem = pl.BlockSpec(memory_space=pltpu.VMEM)
    flops = 4 * rows * QUERY_HEADS * SLOTS * 2 * BLOCK * 2 * HEAD_SIZE
    return pl.pallas_call(
        functools.partial(kernel, dp_size, columns, TURN),
        out_shape=jax.ShapeDtypeStruct(queries.shape, jnp.bfloat16),
        in_specs=[any_space, any_space, any_space, vmem],
        out_specs=vmem,
        scratch_shapes=[
            pltpu.VMEM((SLOTS, 2, KEY_VALUE_HEADS, 2, BLOCK, HEAD_SIZE), jnp.bfloat16),
            pltpu.VMEM((columns + 1, RELAYED, 2, BLOCK, HEAD_SIZE), jnp.bfloat16),
            pltpu.VMEM(queries.shape, jnp.bfloat16),
            pltpu.VMEM((SLOTS, 2 * BLOCK, ndocs), jnp.bfloat16),
            pltpu.VMEM((BLOCK, ndocs), jnp.bfloat16),
            pltpu.VMEM((QUERY_HEADS * BLOCK, HEAD_SIZE), jnp.float32),
            pltpu.VMEM((QUERY_HEADS * BLOCK, 2 * HEAD_SIZE), jnp.float32),
            pltpu.SemaphoreType.DMA((2, KEY_VALUE_HEADS)),
            pltpu.SemaphoreType.DMA(()),
            pltpu.SemaphoreType.DMA((SLOTS, KEY_VALUE_HEADS)),
            pltpu.SemaphoreType.DMA((columns + 1, RELAYED)),
            pltpu.SemaphoreType.DMA((SLOTS, KEY_VALUE_HEADS)),
            pltpu.SemaphoreType.DMA((SLOTS, KEY_VALUE_HEADS)),
            pltpu.SemaphoreType.DMA((columns + 1, RELAYED)),
            pltpu.SemaphoreType.DMA((columns, KEY_VALUE_HEADS)),
            pltpu.SemaphoreType.DMA((SLOTS, KEY_VALUE_HEADS)),
        ],
        compiler_params=pltpu.CompilerParams(
            collective_id=0, has_side_effects=True, vmem_limit_bytes=48 * 1024 * 1024
        ),
        cost_estimate=pl.CostEstimate(
            flops=flops, bytes_accessed=4 * queries.size, transcendentals=0
        ),
    )(queries, keys, values, lengths.reshape(1, ndocs))


def solution(mesh):
    in_specs = (P(("dp", "ctx"), None), P(("dp", "ctx"), None), P(("dp", "ctx"), None), P())
    out_specs = P(("dp", "ctx"), None)
    return jax.shard_map(
        per_device, mesh=mesh, in_specs=in_specs, out_specs=out_specs, check_vma=False
    )
```

```python
import functools
import math

import jax
import jax.numpy as jnp
from jax import lax
from jax.experimental import pallas as pl
from jax.experimental.pallas import tpu as pltpu
from jax.sharding import PartitionSpec as P

HEAD_SIZE = 128
QUERY_HEADS = 32
KEY_VALUE_HEADS = 4
GROUP = QUERY_HEADS // KEY_VALUE_HEADS
BLOCK = 128
SLOTS = 9
TURN = 8
OLDER = (1, 3)
RELAYED = 2
STACK = 2
DIRECT = KEY_VALUE_HEADS - RELAYED
NEG = -1e30
EXPONENT_SCALE = math.log2(math.e) / math.sqrt(HEAD_SIZE)
MESH = pl.DeviceIdType.MESH


def kernel(
    dp_size, columns, turn,
    q_hbm, k_hbm, v_hbm, len_ref, out_ref,
    window, relay, q_ref, hot_ref, qmask_ref, max_ref, acc_ref,
    load_sem, query_sem, recv_sem, relay_recv_sem, pair_recv_sem, row_send_sem, relay_send_sem, older_send_sem, column_send_sem, pair_send_sem,
):
    row = lax.axis_index("dp")
    ctx = lax.axis_index("ctx")
    column, core = ctx // 2, ctx % 2
    chip = row * columns + column
    next_row, last_row = (row + 1) % dp_size, (row + dp_size - 1) % dp_size
    pair = (row, column * 2 + 1 - core)

    def beside(of_row):
        return of_row + turn - 2 * turn * (of_row // turn % 2)

    at_turn = row % turn == turn - 1
    after_turn = row % turn == 0
    relay_to = (beside(row), ctx)
    relayed_to = ((beside(row) + 1) % dp_size, ctx)
    relayed_from = (beside(last_row), ctx)

    def in_row(step):
        return (row, ((column + step) % columns) * 2 + core)

    def load(part, source, head):
        return pltpu.make_async_copy(
            source.at[:, head * HEAD_SIZE:(head + 1) * HEAD_SIZE],
            window.at[0, core, head, part],
            load_sem.at[part, head],
        )

    for head in range(KEY_VALUE_HEADS):
        load(0, k_hbm, head).start()
        load(1, v_hbm, head).start()
    load_q = pltpu.make_async_copy(q_hbm, q_ref, query_sem)
    load_q.start()

    barrier = pltpu.get_barrier_semaphore()
    partners = [in_row(step) for step in range(1, columns)]
    partners += [(next_row, ctx), (last_row, ctx), pair]
    partners += [relay_to, relayed_to, relayed_from]
    for partner in partners:
        pl.semaphore_signal(barrier, inc=1, device_id=partner, device_id_type=MESH)
    pl.semaphore_wait(barrier, len(partners))

    def along_rows(slot, head):
        return pltpu.make_async_remote_copy(
            src_ref=window.at[slot, core, head],
            dst_ref=window.at[slot + columns, core, head],
            send_sem=row_send_sem.at[slot, head],
            recv_sem=recv_sem.at[slot + columns, head],
            device_id=(next_row, ctx),
            device_id_type=MESH,
        )

    def to_relay(slot, head):
        return pltpu.make_async_remote_copy(
            src_ref=window.at[slot, core, head],
            dst_ref=relay.at[slot, head - DIRECT],
            send_sem=row_send_sem.at[slot, head],
            recv_sem=relay_recv_sem.at[slot, head - DIRECT],
            device_id=relay_to,
            device_id_type=MESH,
        )

    def from_relay(slot, head):
        return pltpu.make_async_remote_copy(
            src_ref=relay.at[slot, head - DIRECT],
            dst_ref=window.at[slot + columns, core, head],
            send_sem=relay_send_sem.at[slot, head - DIRECT],
            recv_sem=recv_sem.at[slot + columns, head],
            device_id=relayed_to,
            device_id_type=MESH,
        )

    def send_along_rows(slot, head):
        relayed = at_turn & (head >= DIRECT)

        @pl.when(relayed)
        def _():
            to_relay(slot, head).start()

        @pl.when(jnp.logical_not(relayed))
        def _():
            along_rows(slot, head).start()

    def pass_relayed(slot, head):
        @pl.when(at_turn & (head >= DIRECT))
        def _():
            piece = relay.at[slot, head - DIRECT]
            pltpu.make_async_copy(piece, piece, relay_recv_sem.at[slot, head - DIRECT]).wait()
            from_relay(slot, head).start()

    def along_columns(step, head):
        source = jnp.where(column + step < columns, 0, columns)
        return pltpu.make_async_remote_copy(
            src_ref=window.at[source, core, head],
            dst_ref=window.at[step, core, head],
            send_sem=column_send_sem.at[step, head],
            recv_sem=recv_sem.at[step, head],
            device_id=in_row(step),
            device_id_type=MESH,
        )

    def older_along_columns(step, head):
        source = jnp.where(column + step < columns, columns, 2 * columns)
        return pltpu.make_async_remote_copy(
            src_ref=window.at[source, core, head],
            dst_ref=window.at[step + columns, core, head],
            send_sem=older_send_sem.at[step, head],
            recv_sem=recv_sem.at[step + columns, head],
            device_id=in_row(step),
            device_id_type=MESH,
        )

    def to_pair(slot, head):
        return pltpu.make_async_remote_copy(
            src_ref=window.at[slot, core, head],
            dst_ref=window.at[slot, core, head],
            send_sem=pair_send_sem.at[slot, head],
            recv_sem=pair_recv_sem.at[slot, head],
            device_id=pair,
            device_id_type=MESH,
        )

    def arrived(slot, head):
        piece = window.at[slot, core, head]
        pltpu.make_async_copy(piece, piece, recv_sem.at[slot, head]).wait()

    def pair_arrived(slot, head):
        piece = window.at[slot, 1 - core, head]
        pltpu.make_async_copy(piece, piece, pair_recv_sem.at[slot, head]).wait()

    for head in range(KEY_VALUE_HEADS):
        load(0, k_hbm, head).wait()
        load(1, v_hbm, head).wait()
        if head >= DIRECT:
            send_along_rows(0, head)
        else:
            along_rows(0, head).start()
        for step in (2, 1, 3):
            @pl.when(column + step < columns)
            def _():
                along_columns(step, head).start()
        to_pair(0, head).start()

    lengths = len_ref[...].astype(jnp.float32)
    ndocs = lengths.shape[1]
    sub = lax.broadcasted_iota(jnp.int32, (ndocs, ndocs), 0)
    lane = lax.broadcasted_iota(jnp.int32, (ndocs, ndocs), 1)
    as_column = jnp.sum(jnp.where(sub == lane, lengths, 0.0), axis=1, keepdims=True)
    ends = jnp.sum(jnp.where(sub <= lane, as_column, 0.0), axis=0, keepdims=True)
    begins = ends - lengths
    ends = ends.astype(jnp.int32)
    begins = begins.astype(jnp.int32)
    query_pos = (chip * 2 + core) * BLOCK + lax.broadcasted_iota(jnp.int32, (BLOCK, ndocs), 0)
    same = (query_pos >= begins) & (query_pos < ends)
    qmask_ref[...] = jnp.where(same, 0.0, NEG).astype(jnp.bfloat16)

    @pl.loop(0, SLOTS)
    def _(slot):
        key_pos = (chip - slot) * (2 * BLOCK) + lax.broadcasted_iota(
            jnp.int32, (2 * BLOCK, ndocs), 0
        )
        inside = ((key_pos >= begins) & (key_pos < ends)) | (key_pos < 0)
        hot_ref[slot] = jnp.where(inside, 1.0, 0.0).astype(jnp.bfloat16)

    load_q.wait()

    def attend(slots, head, first, last):
        count = 2 * BLOCK * len(slots)
        blocks = [(s, p) for s in slots for p in (0, 1)]
        key = jnp.concatenate([window[s, p, head, 0] for s, p in blocks], axis=0)
        hot = jnp.concatenate([hot_ref[s] for s in slots], axis=0)
        key = jnp.concatenate([key, hot], axis=1)
        value = jnp.concatenate([window[s, p, head, 1] for s, p in blocks], axis=0)
        value = jnp.concatenate([value, jnp.ones((count, HEAD_SIZE), jnp.bfloat16)], axis=1)
        for inner in range(0, GROUP, STACK):
            heads = [head * GROUP + inner + i for i in range(STACK)]
            spans = [
                pl.ds(pl.multiple_of(n * HEAD_SIZE, HEAD_SIZE), HEAD_SIZE) for n in heads
            ]
            query = jnp.concatenate([q_ref[:, span] for span in spans], axis=0)
            mask = jnp.concatenate([qmask_ref[...]] * STACK, axis=0)
            query = jnp.concatenate([query, mask], axis=1)
            scores = lax.dot_general(
                query, key, (((1,), (1,)), ((), ())), preferred_element_type=jnp.float32
            )
            rows = pl.ds(
                pl.multiple_of(heads[0] * BLOCK, STACK * BLOCK), STACK * BLOCK
            )
            if first:
                key_at = lax.broadcasted_iota(jnp.int32, scores.shape, 1)
                query_at = lax.broadcasted_iota(jnp.int32, scores.shape, 0) % BLOCK
                scores = jnp.where(key_at <= query_at + core * BLOCK, scores, NEG)
            top = jnp.max(scores, axis=1, keepdims=True)
            if first:
                top = jnp.broadcast_to(top, (STACK * BLOCK, HEAD_SIZE))
            else:
                old = max_ref[rows, :]
                top = jnp.maximum(old, top)
            wide = jnp.concatenate([top] * (count // HEAD_SIZE), axis=1)
            weights = jnp.exp2((scores - wide) * EXPONENT_SCALE).astype(jnp.bfloat16)
            total = jnp.dot(weights, value, preferred_element_type=jnp.float32)
            if not first:
                rescale = jnp.exp2((old - top) * EXPONENT_SCALE)
                total = acc_ref[rows, :] * jnp.concatenate([rescale] * 2, axis=1) + total
            if last:
                result = (total[:, :HEAD_SIZE] / total[:, HEAD_SIZE:]).astype(jnp.bfloat16)
                for i, span in enumerate(spans):
                    out_ref[:, span] = result[i * BLOCK:(i + 1) * BLOCK, :]
            else:
                acc_ref[rows, :] = total
                max_ref[rows, :] = top

    def pass_on(head, carry):
        arrived(columns, head)
        for step in (2, 1, 3):
            @pl.when(column + step >= columns)
            def _():
                along_columns(step, head).start()
        for step in OLDER:
            @pl.when(after_turn & (column + step < columns))
            def _():
                older_along_columns(step, head).start()
        send_along_rows(columns, head)
        to_pair(columns, head).start()
        pass_relayed(0, head)
        pair_arrived(0, head)
        attend([0], head, True, False)
        return carry

    def pass_oldest(head, carry):
        pass_relayed(columns, head)
        arrived(2 * columns, head)
        for step in OLDER:
            @pl.when(after_turn & (column + step >= columns))
            def _():
                older_along_columns(step, head).start()
        to_pair(2 * columns, head).start()
        return carry

    def middle(head, carry):
        for slot in (2, 1, 3):
            arrived(slot, head)
            if slot in OLDER:
                @pl.when(jnp.logical_not(at_turn))
                def _():
                    along_rows(slot, head).start()
            else:
                send_along_rows(slot, head)
            to_pair(slot, head).start()
        for slot in (1, 3, 2):
            if slot not in OLDER:
                pass_relayed(slot, head)
        for pair_slots in ([4, 8], [1, 2, 3]):
            for slot in pair_slots:
                pair_arrived(slot, head)
            attend(pair_slots, head, False, False)
        return carry

    def final(head, carry):
        for slot in (5, 7, 6):
            arrived(slot, head)
            to_pair(slot, head).start()
        for slot in (5, 6, 7):
            pair_arrived(slot, head)
        attend([5, 6, 7], head, False, True)
        return carry

    lax.fori_loop(0, KEY_VALUE_HEADS, pass_on, 0)
    lax.fori_loop(0, KEY_VALUE_HEADS, pass_oldest, 0)
    lax.fori_loop(0, KEY_VALUE_HEADS, middle, 0)
    lax.fori_loop(0, KEY_VALUE_HEADS, final, 0)

    def drain(head, carry):
        for slot in range(columns + 1):
            if slot not in OLDER:
                along_rows(slot, head).wait_send()
        for step in OLDER:
            @pl.when(jnp.logical_not(at_turn))
            def _():
                along_rows(step, head).wait_send()

            @pl.when(after_turn)
            def _():
                older_along_columns(step, head).wait_send()
        for step in range(1, columns):
            along_columns(step, head).wait_send()

        @pl.when(at_turn & (head >= DIRECT))
        def _():
            for slot in range(columns + 1):
                if slot not in OLDER:
                    from_relay(slot, head).wait_send()

        for slot in range(SLOTS):
            to_pair(slot, head).wait_send()
        return carry

    lax.fori_loop(0, KEY_VALUE_HEADS, drain, 0)


def per_device(queries, keys, values, lengths):
    columns = lax.axis_size("ctx") // 2
    dp_size = lax.axis_size("dp")
    rows = queries.shape[0]
    ndocs = lengths.shape[0]
    any_space = pl.BlockSpec(memory_space=pl.ANY)
    vmem = pl.BlockSpec(memory_space=pltpu.VMEM)
    flops = 4 * rows * QUERY_HEADS * SLOTS * 2 * BLOCK * 2 * HEAD_SIZE
    return pl.pallas_call(
        functools.partial(kernel, dp_size, columns, TURN),
        out_shape=jax.ShapeDtypeStruct(queries.shape, jnp.bfloat16),
        in_specs=[any_space, any_space, any_space, vmem],
        out_specs=vmem,
        scratch_shapes=[
            pltpu.VMEM((SLOTS, 2, KEY_VALUE_HEADS, 2, BLOCK, HEAD_SIZE), jnp.bfloat16),
            pltpu.VMEM((columns + 1, RELAYED, 2, BLOCK, HEAD_SIZE), jnp.bfloat16),
            pltpu.VMEM(queries.shape, jnp.bfloat16),
            pltpu.VMEM((SLOTS, 2 * BLOCK, ndocs), jnp.bfloat16),
            pltpu.VMEM((BLOCK, ndocs), jnp.bfloat16),
            pltpu.VMEM((QUERY_HEADS * BLOCK, HEAD_SIZE), jnp.float32),
            pltpu.VMEM((QUERY_HEADS * BLOCK, 2 * HEAD_SIZE), jnp.float32),
            pltpu.SemaphoreType.DMA((2, KEY_VALUE_HEADS)),
            pltpu.SemaphoreType.DMA(()),
            pltpu.SemaphoreType.DMA((SLOTS, KEY_VALUE_HEADS)),
            pltpu.SemaphoreType.DMA((columns + 1, RELAYED)),
            pltpu.SemaphoreType.DMA((SLOTS, KEY_VALUE_HEADS)),
            pltpu.SemaphoreType.DMA((SLOTS, KEY_VALUE_HEADS)),
            pltpu.SemaphoreType.DMA((columns + 1, RELAYED)),
            pltpu.SemaphoreType.DMA((columns, KEY_VALUE_HEADS)),
            pltpu.SemaphoreType.DMA((columns, KEY_VALUE_HEADS)),
            pltpu.SemaphoreType.DMA((SLOTS, KEY_VALUE_HEADS)),
        ],
        compiler_params=pltpu.CompilerParams(
            collective_id=0, has_side_effects=True, vmem_limit_bytes=48 * 1024 * 1024
        ),
        cost_estimate=pl.CostEstimate(
            flops=flops, bytes_accessed=4 * queries.size, transcendentals=0
        ),
    )(queries, keys, values, lengths.reshape(1, ndocs))


def solution(mesh):
    in_specs = (P(("dp", "ctx"), None), P(("dp", "ctx"), None), P(("dp", "ctx"), None), P())
    out_specs = P(("dp", "ctx"), None)
    return jax.shard_map(
        per_device, mesh=mesh, in_specs=in_specs, out_specs=out_specs, check_vma=False
    )
```
